128 devices in a mesh: gy: 16 (over z, y_hi, core), gz: 8 (over y_lo, x).
Axes of the slice: x: 4, y: 4 (y_hi: 2, y_lo: 2; y = y_hi * 2 + y_lo), z: 4, core: 2. Of those that a mesh axis runs over, the one named last changes fastest.
Arguments:
- adjoint: float32 [5, 64, 1024, 256], P(None, 'gz', 'gy'), may hold values from -6 to 6
- speed: float32 [64, 1024, 256], P('gz', 'gy'), may hold values from 0.5 to 2
- x_derivative: float32 [256, 256], replicated, may hold values from -0.375 to 0.375
- y_operators: float32 [2, 1024, 1024], replicated, may hold values from -0.1875 to 0.1875
- coupling: float32 [3, 5, 5], replicated, may hold values from -2.5 to 2.5
Outputs:
- advanced: float32 [5, 64, 1024, 256], P(None, 'gz', 'gy')
The draws below stay inside these ranges and needn't reach their ends.
All inputs are finite; a program needn't handle non-finite values.
Results may differ from the reference program's by a relative error of at most 0.0001.
Values sent between devices are 32-bit elements; how exact they have to be, the bound alone decides.
No kernel may reach another device: no remote copies, remote signals or barrier semaphores. Data moves between devices by JAX's collectives and lax.ppermute only.
A program may use at most 128 MiB of HBM per device.

```python
import math
import jax
import jax.numpy as jnp
from jax import lax

FIELDS = 5
NX = 256
NY = 1024
NZ = 64


def block_levels(own_key, dims, shards, low, high):
    def one(position, parts):
        heights = jax.random.uniform(jax.random.fold_in(jax.random.fold_in(own_key, 6), position), (parts,), jnp.float32, low / len(shards), high / len(shards))
        return jnp.repeat(jnp.exp(heights), dims[position] // parts).reshape((-1,) + (1,) * (len(dims) - position - 1))

    level = one(*shards[0])
    for cut in shards[1:]:
        level = level * one(*cut)
    return level


def bell_draw(stream_key, extent, deviation, limit, cuts=(), held_as=jnp.bfloat16):
    gain = block_levels(stream_key, extent, cuts, -0.22, 0.18) if cuts else 1.0
    array = jax.random.normal(stream_key, extent, jnp.float32) * deviation * gain
    return jnp.minimum(jnp.maximum(array, -limit), limit).astype(held_as)


def setup_inputs(seed: int = 0) -> dict:
    key_list = jax.random.split(jax.random.key(seed), 6)
    return {
        "adjoint": bell_draw(key_list[0], (FIELDS, NZ, NY, NX), 1.0, 6.0, ((1, 8), (2, 16)), jnp.float32),
        "speed": jnp.clip(jnp.exp(math.log(2.0) - 1.3862944 * jax.random.uniform(key_list[1], (NZ, NY, NX), jnp.float32) ** block_levels(key_list[1], (NZ, NY, NX), ((0, 8), (1, 16)), -0.2, 0.2)), 0.5, 2.0),
        "x_derivative": bell_draw(key_list[2], (NX, NX), NX ** -0.5, 0.375, (), jnp.float32),
        "y_operators": bell_draw(key_list[3], (2, NY, NY), NY ** -0.5, 0.1875, (), jnp.float32),
        "coupling": bell_draw(key_list[4], (3, FIELDS, FIELDS), FIELDS ** -0.5, 2.5, (), jnp.float32),
    }


stencil = (0.8, -0.2, 4.0 / 105.0, -1.0 / 280.0)
viscous = 0.5
stepping = 0.5


def reference(adjoint, speed, x_derivative, y_operators, coupling):
    highest = lax.Precision.HIGHEST

    def one_field(carry, index):
        advect, curves = carry
        field = lax.dynamic_index_in_dim(adjoint, index, 0, keepdims=False)
        grad_x = jnp.einsum('zyk,xk->zyx', field, x_derivative, precision=highest)
        grad_y = jnp.einsum('yk,zkx->zyx', y_operators[0], field, precision=highest)
        curve_y = jnp.einsum('yk,zkx->zyx', y_operators[1], field, precision=highest)
        grad_z = jnp.zeros_like(field)
        for step, weight in enumerate(stencil):
            shift = step + 1
            grad_z = grad_z + weight * (jnp.roll(field, -shift, axis=0) - jnp.roll(field, shift, axis=0))
        column = lax.dynamic_index_in_dim(coupling, index, 1, keepdims=False)
        advect = (advect + column[0][:, None, None, None] * grad_x[None]
                  + column[1][:, None, None, None] * grad_y[None]
                  + column[2][:, None, None, None] * grad_z[None])
        curves = lax.dynamic_update_index_in_dim(curves, curve_y, index, 0)
        return (advect, curves), None

    start = (jnp.zeros(adjoint.shape, jnp.float32), jnp.zeros(adjoint.shape, jnp.float32))
    (advect, curves), unused = lax.scan(one_field, start, jnp.arange(adjoint.shape[0], dtype=jnp.int32))
    rhs = speed[None] * advect + viscous * curves
    return adjoint + stepping * rhs
```

```python
import jax
import jax.numpy as jnp
from jax import lax
from jax.experimental import pallas as pl
from jax.experimental.pallas import tpu as pltpu
from jax.sharding import PartitionSpec as P


stencil = (0.8, -0.2, 4.0 / 105.0, -1.0 / 280.0)
viscous = 0.5
stepping = 0.5

OFFSETS = ((0, 0), (2, 1), (1, 1), (3, 1), (2, 0), (0, 1), (1, 0), (3, 0))
HALO = len(stencil)


def chip_perm(dz, dy):
    pairs = []
    for i in range(16):
        z, h, c = i // 4, (i // 2) % 2, i % 2
        pairs.append((i, ((z + dz) % 4) * 4 + ((h + dy) % 2) * 2 + c))
    return pairs


CORE_SWAP = [(i, i ^ 1) for i in range(16)]


def split3(value):
    high = value.astype(jnp.bfloat16)
    low = (value - high.astype(jnp.float32)).astype(jnp.bfloat16)
    return high, low


def operator_kernel(core_ref, op_ref, out_ref):
    high, low = split3(op_ref[0, 0, 0])
    n = high.shape[1]
    out_ref[0, 0, :, 0:n] = high
    out_ref[0, 0, :, n : 2 * n] = high
    out_ref[0, 0, :, 2 * n : 3 * n] = low


def own_operators(core, y_operators, chips, rows):
    ops, size, _ = y_operators.shape
    shaped = y_operators.reshape(ops, chips, 2, rows, size)
    out = pl.pallas_call(
        operator_kernel,
        grid_spec=pltpu.PrefetchScalarGridSpec(
            num_scalar_prefetch=1,
            grid=(ops, chips),
            in_specs=[
                pl.BlockSpec((1, 1, 1, rows, size), lambda o, t, core: (o, t, core[0], 0, 0))
            ],
            out_specs=pl.BlockSpec((1, 1, rows, 3 * size), lambda o, t, core: (o, t, 0, 0)),
        ),
        out_shape=jax.ShapeDtypeStruct((ops, chips, rows, 3 * size), jnp.bfloat16),
        name="operators",
        cost_estimate=pl.CostEstimate(
            flops=4 * 1024 * 1024, bytes_accessed=10 * 1024 * 1024, transcendentals=0
        ),
    )(core, shaped)
    return out.reshape(ops * chips * rows, 3 * size)


def lines_kernel(index_ref, coupling_ref, op_ref, *refs):
    count = len(OFFSETS)
    same, other = refs[:count], refs[count : 2 * count]
    speeds = refs[2 * count : 3 * count]
    outs = refs[3 * count : 4 * count]
    parts, grads = refs[4 * count :]
    field = pl.program_id(0)
    fields = pl.num_programs(0)
    rows = same[0].shape[1]
    size = parts.shape[0] // 3
    core = index_ref[2 * count]
    for o in range(count):
        for block, which in ((same[o], core), (other[o], 1 - core)):
            start = pl.multiple_of((index_ref[o] * 2 + which) * rows, rows)
            high, low = split3(block[0])
            parts[pl.ds(start, rows), :] = high
            parts[pl.ds(start + size, rows), :] = low
            parts[pl.ds(start + 2 * size, rows), :] = high
    grads[field] = jnp.dot(op_ref[...], parts[...], preferred_element_type=jnp.float32)

    @pl.when(field == fields - 1)
    def _():
        half = grads.shape[1] // 2
        for o in range(count):
            start = pl.multiple_of(index_ref[count + o] * rows, rows)
            for part in range(0, rows, 16):
                firsts = [grads[g, pl.ds(start + part, 16), :] for g in range(5)]
                speed = speeds[o][0, pl.ds(part, 16), :] * stepping
                for f in range(5):
                    total = coupling_ref[25 + f] * firsts[0]
                    for g in range(1, 5):
                        total = total + coupling_ref[25 + 5 * g + f] * firsts[g]
                    second = grads[f, pl.ds(start + half + part, 16), :]
                    outs[o][f, pl.ds(part, 16), :] = (
                        speed * total + (viscous * stepping) * second
                    )


def line_terms(index, coupling, operators, same, other):
    count = len(OFFSETS)
    fields = same[0].shape[0] - 1
    rows, width = same[0].shape[1:]
    size = operators.shape[1] // 3
    mirrored = [OFFSETS.index(((-dz) % 4, dy)) for dz, dy in OFFSETS]
    piece = pl.BlockSpec((1, rows, width), lambda f, index: (f, 0, 0))
    last = pl.BlockSpec((1, rows, width), lambda f, index: (fields, 0, 0))
    return pl.pallas_call(
        lines_kernel,
        grid_spec=pltpu.PrefetchScalarGridSpec(
            num_scalar_prefetch=1,
            grid=(fields,),
            in_specs=[
                pl.BlockSpec(memory_space=pltpu.SMEM),
                pl.BlockSpec(operators.shape, lambda f, index: (0, 0)),
            ]
            + [piece] * (2 * count)
            + [last] * count,
            out_specs=[pl.BlockSpec((fields, rows, width), lambda f, index: (0, 0, 0))] * count,
            scratch_shapes=[
                pltpu.VMEM((3 * size, width), jnp.bfloat16),
                pltpu.VMEM((fields, operators.shape[0], width), jnp.float32),
            ],
        ),
        out_shape=[jax.ShapeDtypeStruct((fields, rows, width), jnp.float32)] * count,
        name="lines",
        cost_estimate=pl.CostEstimate(
            flops=2 * operators.shape[0] * 3 * size * width * fields,
            bytes_accessed=16 * 1024 * 1024,
            transcendentals=0,
        ),
    )(index, coupling, operators, *same, *other, *[same[m] for m in mirrored])


def local_kernel(coupling_ref, adjoint_ref, low_ref, high_ref, speed_ref, xd_ref, out_ref, gx_ref):
    fields, depth, rows, width = adjoint_ref.shape
    flat = adjoint_ref[...].reshape(fields * depth * rows, width)
    fh, fl = split3(flat)
    xh, xl = split3(xd_ref[...])

    def product(a, b):
        return lax.dot_general(a, b, (((1,), (1,)), ((), ())), preferred_element_type=jnp.float32)

    grad_x = product(fh, xh) + product(fl, xh) + product(fh, xl)
    gx_ref[...] = grad_x.reshape(fields, depth, rows, width)
    for z in range(depth):
        def plane(g, k):
            if k < 0:
                return low_ref[g, HALO + k]
            if k >= depth:
                return high_ref[g, k - depth]
            return adjoint_ref[g, k]

        grad_z = []
        for g in range(fields):
            total = None
            for step, weight in enumerate(stencil):
                term = weight * (plane(g, z + step + 1) - plane(g, z - step - 1))
                total = term if total is None else total + term
            grad_z.append(total)
        speed = speed_ref[z] * stepping
        for f in range(fields):
            total = None
            for g in range(fields):
                term = coupling_ref[5 * g + f] * gx_ref[g, z] + coupling_ref[50 + 5 * g + f] * grad_z[g]
                total = term if total is None else total + term
            out_ref[f, z] = adjoint_ref[f, z] + speed * total


def local_terms(coupling, adjoint, low, high, speed, x_derivative):
    fields, depth, rows, width = adjoint.shape
    step = 8
    return pl.pallas_call(
        local_kernel,
        grid=(rows // step,),
        in_specs=[
            pl.BlockSpec(memory_space=pltpu.SMEM),
            pl.BlockSpec((fields, depth, step, width), lambda r: (0, 0, r, 0)),
            pl.BlockSpec((fields, HALO, step, width), lambda r: (0, 0, r, 0)),
            pl.BlockSpec((fields, HALO, step, width), lambda r: (0, 0, r, 0)),
            pl.BlockSpec((depth, step, width), lambda r: (0, r, 0)),
            pl.BlockSpec((width, width), lambda r: (0, 0)),
        ],
        out_specs=pl.BlockSpec((fields, depth, step, width), lambda r: (0, 0, r, 0)),
        out_shape=jax.ShapeDtypeStruct(adjoint.shape, jnp.float32),
        scratch_shapes=[pltpu.VMEM((fields, depth, step, width), jnp.float32)],
        name="local",
        cost_estimate=pl.CostEstimate(
            flops=6 * fields * depth * rows * width * width,
            bytes_accessed=10 * 1024 * 1024,
            transcendentals=0,
        ),
    )(coupling, adjoint, low, high, speed, x_derivative)


def join_kernel(plane_ref, base_ref, part_ref, out_ref):
    out_ref[:, 0] = base_ref[:, 0] + part_ref[...]


def join(plane, base, part):
    fields, depth, rows, width = base.shape
    spec = pl.BlockSpec((fields, 1, rows, width), lambda i, plane: (0, plane[0], 0, 0))
    return pl.pallas_call(
        join_kernel,
        grid_spec=pltpu.PrefetchScalarGridSpec(
            num_scalar_prefetch=1,
            grid=(1,),
            in_specs=[spec, pl.BlockSpec(part.shape, lambda i, plane: (0, 0, 0))],
            out_specs=spec,
        ),
        out_shape=jax.ShapeDtypeStruct(base.shape, jnp.float32),
        input_output_aliases={1: 0},
        name="join",
        cost_estimate=pl.CostEstimate(
            flops=fields * rows * width, bytes_accessed=1024 * 1024, transcendentals=0
        ),
    )(plane, base, part)


def shards(adjoint, speed, x_derivative, y_operators, coupling):
    fields, depth, rows, width = adjoint.shape
    chips = lax.axis_size("gy") // 2
    assert chips == depth == 8 and y_operators.shape[1] == 16 * rows
    me = lax.axis_index("gy").astype(jnp.int32)
    core, chip = me & 1, lax.shift_right_logical(me, 1)
    targets = [(chip + 2 * dz & 7) ^ dy for dz, dy in OFFSETS]
    sources = [(chip + 8 - 2 * dz & 7) ^ dy for dz, dy in OFFSETS]
    pieces = [
        jnp.concatenate(
            [
                lax.dynamic_index_in_dim(adjoint, t, 1, keepdims=False),
                lax.dynamic_index_in_dim(speed, t, 0, keepdims=True),
            ],
            axis=0,
        )
        for t in targets
    ]
    same = [pieces[0]] + [
        lax.ppermute(pieces[o], "gy", chip_perm(*OFFSETS[o])) for o in range(1, 8)
    ]
    other = [lax.ppermute(block, "gy", CORE_SWAP) for block in same]

    count = lax.axis_size("gz")
    forward = [(i, (i + 1) % count) for i in range(count)]
    backward = [(i, (i - 1) % count) for i in range(count)]
    low = lax.ppermute(adjoint[:, depth - HALO :], "gz", forward)
    high = lax.ppermute(adjoint[:, :HALO], "gz", backward)

    flat = coupling.reshape(-1)
    operators = own_operators(core[None], y_operators, chips, rows)
    index = jnp.stack(sources + targets + [core])
    parts = line_terms(index, flat, operators, same, other)
    result = local_terms(flat, adjoint, low, high, speed, x_derivative)
    result = join(sources[0][None], result, parts[0])
    for o in range(1, 8):
        arrived = lax.ppermute(parts[o], "gy", chip_perm(*OFFSETS[o]))
        result = join(sources[o][None], result, arrived)
    return result


def solution(mesh):
    placed = (P(None, "gz", "gy", None), P("gz", "gy", None), P(), P(), P())
    return jax.shard_map(
        shards, mesh=mesh, in_specs=placed, out_specs=P(None, "gz", "gy", None), check_vma=False
    )
```

```python
import functools

import jax
import jax.numpy as jnp
from jax import lax
from jax.experimental import pallas as pl
from jax.experimental.pallas import tpu as pltpu
from jax.sharding import PartitionSpec as P


stencil = (0.8, -0.2, 4.0 / 105.0, -1.0 / 280.0)
viscous = 0.5
stepping = 0.5

OFFSETS = ((0, 0), (1, 0), (3, 0), (0, 1), (2, 0), (1, 1), (3, 1), (2, 1))
EARLY = 4
HALO = len(stencil)


def chip_perm(dz, dy):
    pairs = []
    for i in range(16):
        z, h, c = i // 4, (i // 2) % 2, i % 2
        pairs.append((i, ((z + dz) % 4) * 4 + ((h + dy) % 2) * 2 + c))
    return pairs


CORE_SWAP = [(i, i ^ 1) for i in range(16)]
MIRRORED = [OFFSETS.index(((-dz) % 4, dy)) for dz, dy in OFFSETS]


def chip_at(me, dz, dy):
    return ((((me >> 2) + dz) & 3) << 1) | (((me >> 1) & 1) ^ dy)


def target(me, o):
    return chip_at(me, OFFSETS[o][0], OFFSETS[o][1])


def source(me, o):
    return chip_at(me, 4 - OFFSETS[o][0], OFFSETS[o][1])


def split3(value):
    high = value.astype(jnp.bfloat16)
    low = (value - high.astype(jnp.float32)).astype(jnp.bfloat16)
    return high, low


def pack_kernel(me_ref, adjoint_ref, speed_ref, *refs):
    count = len(OFFSETS)
    outs = refs[:count]
    hold, arrive, leave = refs[count:]
    fields = adjoint_ref.shape[0]

    def loads(o):
        plane = target(me_ref[0], o)
        return (
            pltpu.make_async_copy(
                adjoint_ref.at[:, plane], hold.at[o, pl.ds(0, fields)], arrive.at[o, 0]
            ),
            pltpu.make_async_copy(speed_ref.at[plane], hold.at[o, fields], arrive.at[o, 1]),
        )

    order = list(range(1, count)) + [0]
    for o in order:
        for copy in loads(o):
            copy.start()
    for o in order:
        for copy in loads(o):
            copy.wait()
        pltpu.make_async_copy(hold.at[o], outs[o], leave.at[o]).start()
    for o in order:
        pltpu.make_async_copy(hold.at[o], outs[o], leave.at[o]).wait()


def pack(me, adjoint, speed):
    fields, _, rows, width = adjoint.shape
    count = len(OFFSETS)
    anywhere = pl.BlockSpec(memory_space=pl.ANY)
    return pl.pallas_call(
        pack_kernel,
        in_specs=[pl.BlockSpec(memory_space=pltpu.SMEM), anywhere, anywhere],
        out_specs=[anywhere] * count,
        out_shape=[jax.ShapeDtypeStruct((fields + 1, rows, width), jnp.float32)] * count,
        scratch_shapes=[
            pltpu.VMEM((count, fields + 1, rows, width), jnp.float32),
            pltpu.SemaphoreType.DMA((count, 2)),
            pltpu.SemaphoreType.DMA((count,)),
        ],
        name="pack",
        cost_estimate=pl.CostEstimate(flops=0, bytes_accessed=6 * 1024 * 1024, transcendentals=0),
    )(me, adjoint, speed)


def operator_kernel(me_ref, op_ref, early_ref, late_ref):
    chips = op_ref.shape[1]
    pair = op_ref.shape[4] // 8
    size = EARLY * pair
    for t in range(chips):
        for o in range(len(OFFSETS)):
            start = pl.multiple_of(source(me_ref[0], o) * pair, pair)
            high, low = split3(op_ref[0, t, 0, :, pl.ds(start, pair)])
            out_ref = early_ref if o < EARLY else late_ref
            at = (o % EARLY) * pair
            out_ref[0, t, :, at : at + pair] = high
            out_ref[0, t, :, size + at : size + at + pair] = high
            out_ref[0, t, :, 2 * size + at : 2 * size + at + pair] = low


def own_operators(me, y_operators, chips, rows):
    ops, size, _ = y_operators.shape
    shaped = y_operators.reshape(ops, chips, 2, rows, size)
    wide = 3 * size // 2
    step = 4
    out_spec = pl.BlockSpec((1, step, rows, wide), lambda o, t, me: (o, t, 0, 0))
    early, late = pl.pallas_call(
        operator_kernel,
        grid_spec=pltpu.PrefetchScalarGridSpec(
            num_scalar_prefetch=1,
            grid=(ops, chips // step),
            in_specs=[
                pl.BlockSpec(
                    (1, step, 1, rows, size), lambda o, t, me: (o, t, me[0] & 1, 0, 0)
                )
            ],
            out_specs=[out_spec] * 2,
        ),
        out_shape=[jax.ShapeDtypeStruct((ops, chips, rows, wide), jnp.bfloat16)] * 2,
        name="operators",
        cost_estimate=pl.CostEstimate(
            flops=4 * 1024 * 1024, bytes_accessed=10 * 1024 * 1024, transcendentals=0
        ),
    )(me, shaped)
    return early.reshape(ops * chips * rows, wide), late.reshape(ops * chips * rows, wide)


def load_parts(core, same, other, parts):
    rows = same[0].shape[1]
    size = parts.shape[0] // 3
    for o in range(EARLY):
        for block, which in ((same[o], core), (other[o], 1 - core)):
            start = pl.multiple_of(o * 2 * rows + which * rows, rows)
            high, low = split3(block[0])
            parts[pl.ds(start, rows), :] = high
            parts[pl.ds(start + size, rows), :] = low
            parts[pl.ds(start + 2 * size, rows), :] = high


def early_kernel(me_ref, op_ref, *refs):
    same, other = refs[:EARLY], refs[EARLY : 2 * EARLY]
    out_ref, parts = refs[2 * EARLY :]
    load_parts(me_ref[0] & 1, same, other, parts)
    out_ref[0] = jnp.dot(op_ref[...], parts[...], preferred_element_type=jnp.float32)


def early_lines(me, operators, same, other):
    fields = same[0].shape[0] - 1
    rows, width = same[0].shape[1:]
    height, size = operators.shape
    piece = pl.BlockSpec((1, rows, width), lambda f, me: (f, 0, 0))
    return pl.pallas_call(
        early_kernel,
        grid_spec=pltpu.PrefetchScalarGridSpec(
            num_scalar_prefetch=1,
            grid=(fields,),
            in_specs=[pl.BlockSpec(operators.shape, lambda f, me: (0, 0))]
            + [piece] * (2 * EARLY),
            out_specs=pl.BlockSpec((1, height, width), lambda f, me: (f, 0, 0)),
            scratch_shapes=[pltpu.VMEM((size, width), jnp.bfloat16)],
        ),
        out_shape=jax.ShapeDtypeStruct((fields, height, width), jnp.float32),
        name="early_lines",
        cost_estimate=pl.CostEstimate(
            flops=2 * height * size * width * fields,
            bytes_accessed=12 * 1024 * 1024,
            transcendentals=0,
        ),
    )(me, operators, *same, *other)


def late_kernel(me_ref, coupling_ref, op_ref, sums_ref, *refs):
    count = len(OFFSETS)
    same, other = refs[:EARLY], refs[EARLY : 2 * EARLY]
    speeds = refs[2 * EARLY : 2 * EARLY + count]
    outs = refs[2 * EARLY + count : 2 * EARLY + 2 * count]
    parts, grads = refs[2 * EARLY + 2 * count :]
    field = pl.program_id(0)
    fields = pl.num_programs(0)
    rows = same[0].shape[1]
    load_parts(me_ref[0] & 1, same, other, parts)
    grads[field] = sums_ref[0] + jnp.dot(
        op_ref[...], parts[...], preferred_element_type=jnp.float32
    )

    @pl.when(field == fields - 1)
    def _():
        half = grads.shape[1] // 2
        for o in range(count):
            start = pl.multiple_of(target(me_ref[0], o) * rows, rows)
            for part in range(0, rows, 16):
                firsts = [grads[g, pl.ds(start + part, 16), :] for g in range(5)]
                speed = speeds[o][0, pl.ds(part, 16), :] * stepping
                for f in range(5):
                    second = grads[f, pl.ds(start + half + part, 16), :]
                    outs[o][f, pl.ds(part, 16), :] = (
                        speed * mixed(coupling_ref, 1, firsts, f)
                        + (viscous * stepping) * second
                    )


def late_lines(me, coupling, operators, sums, same, other, everyone):
    count = len(OFFSETS)
    fields = same[0].shape[0] - 1
    rows, width = same[0].shape[1:]
    height, size = operators.shape
    piece = pl.BlockSpec((1, rows, width), lambda f, me: (f, 0, 0))
    last = pl.BlockSpec((1, rows, width), lambda f, me: (fields, 0, 0))
    return pl.pallas_call(
        late_kernel,
        grid_spec=pltpu.PrefetchScalarGridSpec(
            num_scalar_prefetch=1,
            grid=(fields,),
            in_specs=[
                pl.BlockSpec(memory_space=pltpu.SMEM),
                pl.BlockSpec(operators.shape, lambda f, me: (0, 0)),
                pl.BlockSpec((1, height, width), lambda f, me: (f, 0, 0)),
            ]
            + [piece] * (2 * EARLY)
            + [last] * count,
            out_specs=[pl.BlockSpec((fields, rows, width), lambda f, me: (0, 0, 0))] * count,
            scratch_shapes=[
                pltpu.VMEM((size, width), jnp.bfloat16),
                pltpu.VMEM((fields, height, width), jnp.float32),
            ],
        ),
        out_shape=[jax.ShapeDtypeStruct((fields, rows, width), jnp.float32)] * count,
        name="late_lines",
        cost_estimate=pl.CostEstimate(
            flops=2 * height * size * width * fields,
            bytes_accessed=16 * 1024 * 1024,
            transcendentals=0,
        ),
    )(me, coupling, operators, sums, *same, *other, *[everyone[m] for m in MIRRORED])


def mixed(coupling_ref, axis, grads, f):
    total = coupling_ref[axis, 0, f] * grads[0]
    for g in range(1, len(grads)):
        total = total + coupling_ref[axis, g, f] * grads[g]
    return total


def along_x_kernel(
    coupling_ref, adjoint_ref, speed_ref, xd_ref, out_ref, top_ref, bottom_ref, gx_ref
):
    fields, depth, rows, width = adjoint_ref.shape
    top_ref[...] = adjoint_ref[:, depth - HALO :]
    bottom_ref[...] = adjoint_ref[:, :HALO]
    flat = adjoint_ref[...].reshape(fields * depth * rows, width)
    fh, fl = split3(flat)
    xh, xl = split3(xd_ref[...])

    def product(a, b):
        return lax.dot_general(a, b, (((1,), (1,)), ((), ())), preferred_element_type=jnp.float32)

    grad_x = product(fh, xh) + product(fl, xh) + product(fh, xl)
    gx_ref[...] = grad_x.reshape(fields, depth, rows, width)
    for z in range(depth):
        grads = [gx_ref[g, z] for g in range(fields)]
        speed = speed_ref[z] * stepping
        for f in range(fields):
            out_ref[f, z] = adjoint_ref[f, z] + speed * mixed(coupling_ref, 0, grads, f)


def along_x(coupling, adjoint, speed, x_derivative):
    fields, depth, rows, width = adjoint.shape
    step = 16
    counts = (HALO, HALO)
    return pl.pallas_call(
        along_x_kernel,
        grid=(rows // step,),
        in_specs=[
            pl.BlockSpec(memory_space=pltpu.SMEM),
            pl.BlockSpec((fields, depth, step, width), lambda r: (0, 0, r, 0)),
            pl.BlockSpec((depth, step, width), lambda r: (0, r, 0)),
            pl.BlockSpec((width, width), lambda r: (0, 0)),
        ],
        out_specs=[
            pl.BlockSpec((fields, depth, step, width), lambda r: (0, 0, r, 0)),
        ]
        + [
            pl.BlockSpec((fields, count, step, width), lambda r: (0, 0, r, 0)) for count in counts
        ],
        out_shape=[jax.ShapeDtypeStruct(adjoint.shape, jnp.float32)]
        + [jax.ShapeDtypeStruct((fields, count, rows, width), jnp.float32) for count in counts],
        scratch_shapes=[pltpu.VMEM((fields, depth, step, width), jnp.float32)],
        name="along_x",
        cost_estimate=pl.CostEstimate(
            flops=6 * fields * depth * rows * width * width,
            bytes_accessed=6 * 1024 * 1024,
            transcendentals=0,
        ),
    )(coupling, adjoint, speed, x_derivative)


def along_z_kernel(coupling_ref, base_ref, adjoint_ref, low_ref, high_ref, speed_ref, out_ref):
    fields, depth, _, _ = adjoint_ref.shape

    def plane(g, k):
        if k < 0:
            return low_ref[g, HALO + k]
        if k >= depth:
            return high_ref[g, k - depth]
        return adjoint_ref[g, k]

    for z in range(depth):
        grads = []
        for g in range(fields):
            total = None
            for step, weight in enumerate(stencil):
                term = weight * (plane(g, z + step + 1) - plane(g, z - step - 1))
                total = term if total is None else total + term
            grads.append(total)
        speed = speed_ref[z] * stepping
        for f in range(fields):
            out_ref[f, z] = base_ref[f, z] + speed * mixed(coupling_ref, 2, grads, f)


def along_z(coupling, base, adjoint, low, high, speed):
    fields, depth, rows, width = adjoint.shape
    step = 8
    whole = pl.BlockSpec((fields, depth, step, width), lambda r: (0, 0, r, 0))
    side = pl.BlockSpec((fields, HALO, step, width), lambda r: (0, 0, r, 0))
    return pl.pallas_call(
        along_z_kernel,
        grid=(rows // step,),
        in_specs=[
            pl.BlockSpec(memory_space=pltpu.SMEM),
            whole,
            whole,
            side,
            side,
            pl.BlockSpec((depth, step, width), lambda r: (0, r, 0)),
        ],
        out_specs=whole,
        out_shape=jax.ShapeDtypeStruct(adjoint.shape, jnp.float32),
        input_output_aliases={1: 0},
        name="along_z",
        cost_estimate=pl.CostEstimate(
            flops=70 * fields * depth * rows * width,
            bytes_accessed=12 * 1024 * 1024,
            transcendentals=0,
        ),
    )(coupling, base, adjoint, low, high, speed)


def join_kernel(me_ref, base_ref, *refs, where):
    parts, (out_ref, hold, extra, arrive, leave) = refs[:-5], refs[-5:]
    fields = base_ref.shape[0]

    def load(k):
        plane = source(me_ref[0], where[k])
        return pltpu.make_async_copy(base_ref.at[:, plane], hold.at[k], arrive.at[k])

    def fetch(k):
        return pltpu.make_async_copy(parts[k], extra.at[k], arrive.at[len(where) + k])

    def store(k):
        plane = source(me_ref[0], where[k])
        return pltpu.make_async_copy(hold.at[k], out_ref.at[:, plane], leave.at[k])

    for k in range(len(where)):
        load(k).start()
        fetch(k).start()
    for k in range(len(where)):
        load(k).wait()
        fetch(k).wait()
        for f in range(fields):
            hold[k, f] = hold[k, f] + extra[k, f]
        store(k).start()
    for k in range(len(where)):
        store(k).wait()


def join(me, base, parts, where):
    fields, _, rows, width = base.shape
    count = len(where)
    anywhere = pl.BlockSpec(memory_space=pl.ANY)
    return pl.pallas_call(
        functools.partial(join_kernel, where=where),
        in_specs=[pl.BlockSpec(memory_space=pltpu.SMEM), anywhere] + [anywhere] * count,
        out_specs=anywhere,
        out_shape=jax.ShapeDtypeStruct(base.shape, jnp.float32),
        scratch_shapes=[
            pltpu.VMEM((count, fields, rows, width), jnp.float32),
            pltpu.VMEM((count, fields, rows, width), jnp.float32),
            pltpu.SemaphoreType.DMA((2 * count,)),
            pltpu.SemaphoreType.DMA((count,)),
        ],
        input_output_aliases={1: 0},
        name="join",
        cost_estimate=pl.CostEstimate(
            flops=count * fields * rows * width,
            bytes_accessed=count * 1024 * 1024,
            transcendentals=0,
        ),
    )(me, base, *parts)


def shards(adjoint, speed, x_derivative, y_operators, coupling):
    _, depth, rows, _ = adjoint.shape
    chips = lax.axis_size("gy") // 2
    assert chips == depth == 8 and y_operators.shape[1] == 16 * rows
    me = lax.axis_index("gy").astype(jnp.int32)[None]
    pieces = pack(me, adjoint, speed)
    same = [pieces[0]]
    for o in range(1, 8):
        same.append(lax.ppermute(pieces[o], "gy", chip_perm(*OFFSETS[o])))
    other = []
    for o in range(8):
        other.append(lax.ppermute(same[o], "gy", CORE_SWAP))

    result, top, bottom = along_x(coupling, adjoint, speed, x_derivative)
    count = lax.axis_size("gz")
    forward = [(i, (i + 1) % count) for i in range(count)]
    backward = [(i, (i - 1) % count) for i in range(count)]
    low = lax.ppermute(top, "gz", forward)
    high = lax.ppermute(bottom, "gz", backward)

    early, late = own_operators(me, y_operators, chips, rows)
    sums = early_lines(me, early, same[:EARLY], other[:EARLY])
    parts = late_lines(me, coupling, late, sums, same[EARLY:], other[EARLY:], same)
    result = along_z(coupling, result, adjoint, low, high, speed)
    arrived = [parts[0]]
    for o in range(1, 8):
        arrived.append(lax.ppermute(parts[o], "gy", chip_perm(*OFFSETS[o])))
    for where in ((0, 1, 2), (3, 4), (5, 6, 7)):
        result = join(me, result, [arrived[o] for o in where], where)
    return result


def solution(mesh):
    placed = (P(None, "gz", "gy", None), P("gz", "gy", None), P(), P(), P())

    return jax.shard_map(
        shards, mesh=mesh, in_specs=placed, out_specs=P(None, "gz", "gy", None), check_vma=False
    )
```

```python
import functools

import jax
import jax.numpy as jnp
from jax import lax
from jax.experimental import pallas as pl
from jax.experimental.pallas import tpu as pltpu
from jax.sharding import PartitionSpec as P


stencil = (0.8, -0.2, 4.0 / 105.0, -1.0 / 280.0)
viscous = 0.5
stepping = 0.5

OFFSETS = ((0, 0), (1, 0), (3, 0), (0, 1), (2, 0), (1, 1), (3, 1), (2, 1))
EARLY = 4
HALO = len(stencil)


def chip_perm(dz, dy):
    pairs = []
    for i in range(16):
        z, h, c = i // 4, (i // 2) % 2, i % 2
        pairs.append((i, ((z + dz) % 4) * 4 + ((h + dy) % 2) * 2 + c))
    return pairs


CORE_SWAP = [(i, i ^ 1) for i in range(16)]
MIRRORED = [OFFSETS.index(((-dz) % 4, dy)) for dz, dy in OFFSETS]


def chip_at(me, dz, dy):
    return ((((me >> 2) + dz) & 3) << 1) | (((me >> 1) & 1) ^ dy)


def target(me, o):
    return chip_at(me, OFFSETS[o][0], OFFSETS[o][1])


def source(me, o):
    return chip_at(me, 4 - OFFSETS[o][0], OFFSETS[o][1])


def split3(value):
    high = value.astype(jnp.bfloat16)
    low = (value - high.astype(jnp.float32)).astype(jnp.bfloat16)
    return high, low


def pack_kernel(me_ref, adjoint_ref, speed_ref, *refs):
    count = len(OFFSETS)
    outs = refs[:count]
    hold, arrive, leave = refs[count:]
    fields = adjoint_ref.shape[0]

    def loads(o):
        plane = target(me_ref[0], o)
        return (
            pltpu.make_async_copy(
                adjoint_ref.at[:, plane], hold.at[o, pl.ds(0, fields)], arrive.at[o, 0]
            ),
            pltpu.make_async_copy(speed_ref.at[plane], hold.at[o, fields], arrive.at[o, 1]),
        )

    order = list(range(1, count)) + [0]
    for o in order:
        for copy in loads(o):
            copy.start()
    for o in order:
        for copy in loads(o):
            copy.wait()
        pltpu.make_async_copy(hold.at[o], outs[o], leave.at[o]).start()
    for o in order:
        pltpu.make_async_copy(hold.at[o], outs[o], leave.at[o]).wait()


def pack(me, adjoint, speed):
    fields, _, rows, width = adjoint.shape
    count = len(OFFSETS)
    anywhere = pl.BlockSpec(memory_space=pl.ANY)
    return pl.pallas_call(
        pack_kernel,
        in_specs=[pl.BlockSpec(memory_space=pltpu.SMEM), anywhere, anywhere],
        out_specs=[anywhere] * count,
        out_shape=[jax.ShapeDtypeStruct((fields + 1, rows, width), jnp.float32)] * count,
        scratch_shapes=[
            pltpu.VMEM((count, fields + 1, rows, width), jnp.float32),
            pltpu.SemaphoreType.DMA((count, 2)),
            pltpu.SemaphoreType.DMA((count,)),
        ],
        name="pack",
        cost_estimate=pl.CostEstimate(flops=0, bytes_accessed=6 * 1024 * 1024, transcendentals=0),
    )(me, adjoint, speed)


def operator_kernel(me_ref, op_ref, early_ref, late_ref):
    chips = op_ref.shape[1]
    pair = op_ref.shape[4] // 8
    size = EARLY * pair
    for t in range(chips):
        for o in range(len(OFFSETS)):
            start = pl.multiple_of(source(me_ref[0], o) * pair, pair)
            high, low = split3(op_ref[0, t, 0, :, pl.ds(start, pair)])
            out_ref = early_ref if o < EARLY else late_ref
            at = (o % EARLY) * pair
            out_ref[0, t, :, at : at + pair] = high
            out_ref[0, t, :, size + at : size + at + pair] = high
            out_ref[0, t, :, 2 * size + at : 2 * size + at + pair] = low


def own_operators(me, y_operators, chips, rows):
    ops, size, _ = y_operators.shape
    shaped = y_operators.reshape(ops, chips, 2, rows, size)
    wide = 3 * size // 2
    step = 4
    out_spec = pl.BlockSpec((1, step, rows, wide), lambda o, t, me: (o, t, 0, 0))
    early, late = pl.pallas_call(
        operator_kernel,
        grid_spec=pltpu.PrefetchScalarGridSpec(
            num_scalar_prefetch=1,
            grid=(ops, chips // step),
            in_specs=[
                pl.BlockSpec(
                    (1, step, 1, rows, size), lambda o, t, me: (o, t, me[0] & 1, 0, 0)
                )
            ],
            out_specs=[out_spec] * 2,
        ),
        out_shape=[jax.ShapeDtypeStruct((ops, chips, rows, wide), jnp.bfloat16)] * 2,
        name="operators",
        cost_estimate=pl.CostEstimate(
            flops=4 * 1024 * 1024, bytes_accessed=10 * 1024 * 1024, transcendentals=0
        ),
    )(me, shaped)
    return early.reshape(ops * chips * rows, wide), late.reshape(ops * chips * rows, wide)


def load_parts(core, same, other, parts):
    rows = same[0].shape[1]
    size = parts.shape[0] // 3
    for o in range(EARLY):
        for block, which in ((same[o], core), (other[o], 1 - core)):
            start = pl.multiple_of(o * 2 * rows + which * rows, rows)
            high, low = split3(block[0])
            parts[pl.ds(start, rows), :] = high
            parts[pl.ds(start + size, rows), :] = low
            parts[pl.ds(start + 2 * size, rows), :] = high


def early_kernel(me_ref, op_ref, *refs):
    same, other = refs[:EARLY], refs[EARLY : 2 * EARLY]
    out_ref, parts = refs[2 * EARLY :]
    load_parts(me_ref[0] & 1, same, other, parts)
    out_ref[0] = jnp.dot(op_ref[...], parts[...], preferred_element_type=jnp.float32)


def early_lines(me, operators, same, other):
    fields = same[0].shape[0] - 1
    rows, width = same[0].shape[1:]
    height, size = operators.shape
    piece = pl.BlockSpec((1, rows, width), lambda f, me: (f, 0, 0))
    return pl.pallas_call(
        early_kernel,
        grid_spec=pltpu.PrefetchScalarGridSpec(
            num_scalar_prefetch=1,
            grid=(fields,),
            in_specs=[pl.BlockSpec(operators.shape, lambda f, me: (0, 0))]
            + [piece] * (2 * EARLY),
            out_specs=pl.BlockSpec((1, height, width), lambda f, me: (f, 0, 0)),
            scratch_shapes=[pltpu.VMEM((size, width), jnp.bfloat16)],
        ),
        out_shape=jax.ShapeDtypeStruct((fields, height, width), jnp.float32),
        name="early_lines",
        cost_estimate=pl.CostEstimate(
            flops=2 * height * size * width * fields,
            bytes_accessed=12 * 1024 * 1024,
            transcendentals=0,
        ),
    )(me, operators, *same, *other)


def late_kernel(me_ref, coupling_ref, op_ref, sums_ref, *refs):
    count = len(OFFSETS)
    same, other = refs[:EARLY], refs[EARLY : 2 * EARLY]
    speeds = refs[2 * EARLY : 2 * EARLY + count]
    outs = refs[2 * EARLY + count : 2 * EARLY + 2 * count]
    parts, grads = refs[2 * EARLY + 2 * count :]
    field = pl.program_id(0)
    fields = pl.num_programs(0)
    rows = same[0].shape[1]
    load_parts(me_ref[0] & 1, same, other, parts)
    grads[field] = sums_ref[0] + jnp.dot(
        op_ref[...], parts[...], preferred_element_type=jnp.float32
    )

    @pl.when(field == fields - 1)
    def _():
        half = grads.shape[1] // 2
        for o in range(count):
            start = pl.multiple_of(target(me_ref[0], o) * rows, rows)
            for part in range(0, rows, 16):
                firsts = [grads[g, pl.ds(start + part, 16), :] for g in range(5)]
                speed = speeds[o][0, pl.ds(part, 16), :] * stepping
                for f in range(5):
                    second = grads[f, pl.ds(start + half + part, 16), :]
                    outs[o][f, pl.ds(part, 16), :] = (
                        speed * mixed(coupling_ref, 1, firsts, f)
                        + (viscous * stepping) * second
                    )


def late_lines(me, coupling, operators, sums, same, other, everyone):
    count = len(OFFSETS)
    fields = same[0].shape[0] - 1
    rows, width = same[0].shape[1:]
    height, size = operators.shape
    piece = pl.BlockSpec((1, rows, width), lambda f, me: (f, 0, 0))
    last = pl.BlockSpec((1, rows, width), lambda f, me: (fields, 0, 0))
    return pl.pallas_call(
        late_kernel,
        grid_spec=pltpu.PrefetchScalarGridSpec(
            num_scalar_prefetch=1,
            grid=(fields,),
            in_specs=[
                pl.BlockSpec(memory_space=pltpu.SMEM),
                pl.BlockSpec(operators.shape, lambda f, me: (0, 0)),
                pl.BlockSpec((1, height, width), lambda f, me: (f, 0, 0)),
            ]
            + [piece] * (2 * EARLY)
            + [last] * count,
            out_specs=[pl.BlockSpec((fields, rows, width), lambda f, me: (0, 0, 0))] * count,
            scratch_shapes=[
                pltpu.VMEM((size, width), jnp.bfloat16),
                pltpu.VMEM((fields, height, width), jnp.float32),
            ],
        ),
        out_shape=[jax.ShapeDtypeStruct((fields, rows, width), jnp.float32)] * count,
        name="late_lines",
        cost_estimate=pl.CostEstimate(
            flops=2 * height * size * width * fields,
            bytes_accessed=16 * 1024 * 1024,
            transcendentals=0,
        ),
    )(me, coupling, operators, sums, *same, *other, *[everyone[m] for m in MIRRORED])


def mixed(coupling_ref, axis, grads, f):
    total = coupling_ref[0, axis, f] * grads[0]
    for g in range(1, len(grads)):
        total = total + coupling_ref[g, axis, f] * grads[g]
    return total


def edges_kernel(column_ref, adjoint_ref, top_ref, bottom_ref, near_ref, far_ref, hold, arrive, leave):
    fields, depth = adjoint_ref.shape[:2]
    half = HALO // 2
    edge = jnp.where(column_ref[0] == 3, depth - HALO, 0)

    def load(f):
        return pltpu.make_async_copy(adjoint_ref.at[f], hold.at[f], arrive.at[f])

    def stores(f):
        return [
            pltpu.make_async_copy(hold.at[f, pl.ds(start, size)], out.at[f], leave.at[f, k])
            for k, (out, start, size) in enumerate(
                (
                    (near_ref, edge, half),
                    (far_ref, edge + half, half),
                    (top_ref, depth - HALO, HALO),
                    (bottom_ref, 0, HALO),
                )
            )
        ]

    for f in range(fields):
        load(f).start()
    for f in range(fields):
        load(f).wait()
        for copy in stores(f):
            copy.start()
    for f in range(fields):
        for copy in stores(f):
            copy.wait()


def edges(column, adjoint):
    fields, _, rows, width = adjoint.shape
    counts = (HALO, HALO, HALO // 2, HALO // 2)
    anywhere = pl.BlockSpec(memory_space=pl.ANY)
    return pl.pallas_call(
        edges_kernel,
        in_specs=[pl.BlockSpec(memory_space=pltpu.SMEM), anywhere],
        out_specs=[anywhere] * len(counts),
        out_shape=[jax.ShapeDtypeStruct((fields, count, rows, width), jnp.float32) for count in counts],
        scratch_shapes=[
            pltpu.VMEM(adjoint.shape, jnp.float32),
            pltpu.SemaphoreType.DMA((fields,)),
            pltpu.SemaphoreType.DMA((fields, len(counts))),
        ],
        name="edges",
        cost_estimate=pl.CostEstimate(flops=0, bytes_accessed=7 * 1024 * 1024, transcendentals=0),
    )(column, adjoint)


def local_kernel(
    column_ref, coupling_ref, adjoint_ref, low_ref, high_ref, near_ref, far_ref, speed_ref,
    xd_ref, out_ref, full_ref, gx_ref,
):
    fields, depth, rows, width = adjoint_ref.shape
    half = HALO // 2
    first, last = column_ref[0] == 0, column_ref[0] == 3
    for g in range(fields):
        for k in range(HALO):
            wrapped = near_ref[g, k] if k < half else far_ref[g, k - half]
            full_ref[g, k] = jnp.where(first, wrapped, low_ref[g, k])
            full_ref[g, HALO + k] = jnp.where(last, wrapped, high_ref[g, k])
    flat = adjoint_ref[...].reshape(fields * depth * rows, width)
    fh, fl = split3(flat)
    xh, xl = split3(xd_ref[...])

    def product(a, b):
        return lax.dot_general(a, b, (((1,), (1,)), ((), ())), preferred_element_type=jnp.float32)

    grad_x = product(fh, xh) + product(fl, xh) + product(fh, xl)
    gx_ref[...] = grad_x.reshape(fields, depth, rows, width)

    def plane(g, k):
        if k < 0:
            return full_ref[g, HALO + k]
        if k >= depth:
            return full_ref[g, HALO + k - depth]
        return adjoint_ref[g, k]

    for z in range(depth):
        grads = []
        for g in range(fields):
            total = None
            for step, weight in enumerate(stencil):
                term = weight * (plane(g, z + step + 1) - plane(g, z - step - 1))
                total = term if total is None else total + term
            grads.append(total)
        firsts = [gx_ref[g, z] for g in range(fields)]
        speed = speed_ref[z] * stepping
        for f in range(fields):
            total = mixed(coupling_ref, 0, firsts, f) + mixed(coupling_ref, 2, grads, f)
            out_ref[f, z] = adjoint_ref[f, z] + speed * total


def local_terms(column, coupling, adjoint, low, high, near, far, speed, x_derivative):
    fields, depth, rows, width = adjoint.shape
    step = 8
    whole = pl.BlockSpec((fields, depth, step, width), lambda r: (0, 0, r, 0))
    side = pl.BlockSpec((fields, HALO, step, width), lambda r: (0, 0, r, 0))
    part = pl.BlockSpec((fields, HALO // 2, step, width), lambda r: (0, 0, r, 0))
    return pl.pallas_call(
        local_kernel,
        grid=(rows // step,),
        in_specs=[
            pl.BlockSpec(memory_space=pltpu.SMEM),
            pl.BlockSpec(memory_space=pltpu.SMEM),
            whole,
            side,
            side,
            part,
            part,
            pl.BlockSpec((depth, step, width), lambda r: (0, r, 0)),
            pl.BlockSpec((width, width), lambda r: (0, 0)),
        ],
        out_specs=whole,
        out_shape=jax.ShapeDtypeStruct(adjoint.shape, jnp.float32),
        scratch_shapes=[
            pltpu.VMEM((fields, 2 * HALO, step, width), jnp.float32),
            pltpu.VMEM((fields, depth, step, width), jnp.float32),
        ],
        name="local",
        cost_estimate=pl.CostEstimate(
            flops=6 * fields * depth * rows * width * width,
            bytes_accessed=12 * 1024 * 1024,
            transcendentals=0,
        ),
    )(column, coupling, adjoint, low, high, near, far, speed, x_derivative)


def join_kernel(me_ref, base_ref, *refs, where):
    parts, (out_ref, hold, extra, arrive, leave) = refs[:-5], refs[-5:]
    fields = base_ref.shape[0]

    def load(k):
        plane = source(me_ref[0], where[k])
        return pltpu.make_async_copy(base_ref.at[:, plane], hold.at[k], arrive.at[k])

    def fetch(k):
        return pltpu.make_async_copy(parts[k], extra.at[k], arrive.at[len(where) + k])

    def store(k):
        plane = source(me_ref[0], where[k])
        return pltpu.make_async_copy(hold.at[k], out_ref.at[:, plane], leave.at[k])

    for k in range(len(where)):
        load(k).start()
        fetch(k).start()
    for k in range(len(where)):
        load(k).wait()
        fetch(k).wait()
        for f in range(fields):
            hold[k, f] = hold[k, f] + extra[k, f]
        store(k).start()
    for k in range(len(where)):
        store(k).wait()


def join(me, base, parts, where):
    fields, _, rows, width = base.shape
    count = len(where)
    anywhere = pl.BlockSpec(memory_space=pl.ANY)
    return pl.pallas_call(
        functools.partial(join_kernel, where=where),
        in_specs=[pl.BlockSpec(memory_space=pltpu.SMEM), anywhere] + [anywhere] * count,
        out_specs=anywhere,
        out_shape=jax.ShapeDtypeStruct(base.shape, jnp.float32),
        scratch_shapes=[
            pltpu.VMEM((count, fields, rows, width), jnp.float32),
            pltpu.VMEM((count, fields, rows, width), jnp.float32),
            pltpu.SemaphoreType.DMA((2 * count,)),
            pltpu.SemaphoreType.DMA((count,)),
        ],
        input_output_aliases={1: 0},
        name="join",
        cost_estimate=pl.CostEstimate(
            flops=count * fields * rows * width,
            bytes_accessed=count * 1024 * 1024,
            transcendentals=0,
        ),
    )(me, base, *parts)


def shards(adjoint, speed, x_derivative, y_operators, coupling):
    _, depth, rows, _ = adjoint.shape
    chips = lax.axis_size("gy") // 2
    assert chips == depth == 8 and y_operators.shape[1] == 16 * rows
    coupling = jnp.transpose(coupling, (1, 0, 2))
    me = lax.axis_index("gy").astype(jnp.int32)[None]
    column = (lax.axis_index("gz").astype(jnp.int32) & 3)[None]
    pieces = pack(me, adjoint, speed)
    same = [pieces[0]]
    for o in range(1, 8):
        same.append(lax.ppermute(pieces[o], "gy", chip_perm(*OFFSETS[o])))
    other = []
    for o in range(8):
        other.append(lax.ppermute(same[o], "gy", CORE_SWAP))

    top, bottom, near, far = edges(column, adjoint)
    runs = [4 * r for r in range(lax.axis_size("gz") // 4)]
    near = lax.ppermute(near, "gz", [p for r in runs for p in ((r + 3, r), (r, r + 3))])
    far = lax.ppermute(far, "gz", [p for r in runs for p in ((r + 3, r + 1), (r, r + 2))])
    low = lax.ppermute(top, "gz", [(r + x, r + (x + 1) % 4) for r in runs for x in range(4)])
    high = lax.ppermute(bottom, "gz", [(r + (x + 1) % 4, r + x) for r in runs for x in range(4)])
    ends = (column[0] == 0) | (column[0] == 3)
    crossing = jnp.where(ends, near, far)
    near = lax.ppermute(crossing, "gz", [(r + x, (r ^ 4) + x) for r in runs for x in range(4)])
    far = lax.ppermute(near, "gz", [p for r in runs for p in ((r + 1, r), (r + 2, r + 3))])

    early, late = own_operators(me, y_operators, chips, rows)
    sums = early_lines(me, early, same[:EARLY], other[:EARLY])
    parts = late_lines(me, coupling, late, sums, same[EARLY:], other[EARLY:], same)
    result = local_terms(
        column, coupling, adjoint, low, high, near, far, speed, x_derivative
    )
    arrived = [parts[0]]
    for o in range(1, 8):
        arrived.append(lax.ppermute(parts[o], "gy", chip_perm(*OFFSETS[o])))
    for where in ((0, 1, 2), (3, 4), (5, 6, 7)):
        result = join(me, result, [arrived[o] for o in where], where)
    return result


def solution(mesh):
    placed = (P(None, "gz", "gy", None), P("gz", "gy", None), P(), P(), P())

    return jax.shard_map(
        shards, mesh=mesh, in_specs=placed, out_specs=P(None, "gz", "gy", None), check_vma=False
    )
```

```python
import functools

import jax
import jax.numpy as jnp
from jax import lax
from jax.experimental import pallas as pl
from jax.experimental.pallas import tpu as pltpu
from jax.sharding import PartitionSpec as P


stencil = (0.8, -0.2, 4.0 / 105.0, -1.0 / 280.0)
viscous = 0.5
stepping = 0.5

OFFSETS = ((0, 0), (1, 0), (3, 0), (0, 1), (2, 0), (1, 1), (3, 1), (2, 1))
EARLY = 4
FIRST = 4
LATER = ((4, 5, 6, 7),)
HALO = len(stencil)


def chip_perm(dz, dy):
    pairs = []
    for i in range(16):
        z, h, c = i // 4, (i // 2) % 2, i % 2
        pairs.append((i, ((z + dz) % 4) * 4 + ((h + dy) % 2) * 2 + c))
    return pairs


CORE_SWAP = [(i, i ^ 1) for i in range(16)]
MIRRORED = [OFFSETS.index(((-dz) % 4, dy)) for dz, dy in OFFSETS]


def chip_at(me, dz, dy):
    return ((((me >> 2) + dz) & 3) << 1) | (((me >> 1) & 1) ^ dy)


def target(me, o):
    return chip_at(me, OFFSETS[o][0], OFFSETS[o][1])


def source(me, o):
    return chip_at(me, 4 - OFFSETS[o][0], OFFSETS[o][1])


def split3(value):
    high = value.astype(jnp.bfloat16)
    low = (value - high.astype(jnp.float32)).astype(jnp.bfloat16)
    return high, low


def pack_kernel(me_ref, adjoint_ref, speed_ref, *refs):
    count = len(OFFSETS)
    outs = refs[:count]
    hold, arrive, leave = refs[count:]
    fields = adjoint_ref.shape[0]

    def loads(o):
        plane = target(me_ref[0], o)
        return (
            pltpu.make_async_copy(
                adjoint_ref.at[:, plane], hold.at[o, pl.ds(0, fields)], arrive.at[o, 0]
            ),
            pltpu.make_async_copy(speed_ref.at[plane], hold.at[o, fields], arrive.at[o, 1]),
        )

    order = list(range(1, count)) + [0]
    for o in order:
        for copy in loads(o):
            copy.start()
    for o in order:
        for copy in loads(o):
            copy.wait()
        pltpu.make_async_copy(hold.at[o], outs[o], leave.at[o]).start()
    for o in order:
        pltpu.make_async_copy(hold.at[o], outs[o], leave.at[o]).wait()


def pack(me, adjoint, speed):
    fields, _, rows, width = adjoint.shape
    count = len(OFFSETS)
    anywhere = pl.BlockSpec(memory_space=pl.ANY)
    return pl.pallas_call(
        pack_kernel,
        in_specs=[pl.BlockSpec(memory_space=pltpu.SMEM), anywhere, anywhere],
        out_specs=[anywhere] * count,
        out_shape=[jax.ShapeDtypeStruct((fields + 1, rows, width), jnp.float32)] * count,
        scratch_shapes=[
            pltpu.VMEM((count, fields + 1, rows, width), jnp.float32),
            pltpu.SemaphoreType.DMA((count, 2)),
            pltpu.SemaphoreType.DMA((count,)),
        ],
        name="pack",
        cost_estimate=pl.CostEstimate(flops=0, bytes_accessed=6 * 1024 * 1024, transcendentals=0),
    )(me, adjoint, speed)


def operator_kernel(me_ref, op_ref, early_ref, late_ref):
    chips = op_ref.shape[1]
    pair = op_ref.shape[4] // 8
    size = EARLY * pair
    for t in range(chips):
        for o in range(len(OFFSETS)):
            start = pl.multiple_of(source(me_ref[0], o) * pair, pair)
            high, low = split3(op_ref[0, t, 0, :, pl.ds(start, pair)])
            out_ref = early_ref if o < EARLY else late_ref
            at = (o % EARLY) * pair
            out_ref[0, t, :, at : at + pair] = high
            out_ref[0, t, :, size + at : size + at + pair] = high
            out_ref[0, t, :, 2 * size + at : 2 * size + at + pair] = low


def own_operators(me, y_operators, chips, rows):
    ops, size, _ = y_operators.shape
    shaped = y_operators.reshape(ops, chips, 2, rows, size)
    wide = 3 * size // 2
    step = 4
    out_spec = pl.BlockSpec((1, step, rows, wide), lambda o, t, me: (o, t, 0, 0))
    early, late = pl.pallas_call(
        operator_kernel,
        grid_spec=pltpu.PrefetchScalarGridSpec(
            num_scalar_prefetch=1,
            grid=(ops, chips // step),
            in_specs=[
                pl.BlockSpec(
                    (1, step, 1, rows, size), lambda o, t, me: (o, t, me[0] & 1, 0, 0)
                )
            ],
            out_specs=[out_spec] * 2,
        ),
        out_shape=[jax.ShapeDtypeStruct((ops, chips, rows, wide), jnp.bfloat16)] * 2,
        name="operators",
        cost_estimate=pl.CostEstimate(
            flops=4 * 1024 * 1024, bytes_accessed=10 * 1024 * 1024, transcendentals=0
        ),
    )(me, shaped)
    return early.reshape(ops * chips * rows, wide), late.reshape(ops * chips * rows, wide)


def load_parts(core, same, other, parts):
    rows = same[0].shape[1]
    size = parts.shape[0] // 3
    for o in range(EARLY):
        for block, which in ((same[o], core), (other[o], 1 - core)):
            start = pl.multiple_of(o * 2 * rows + which * rows, rows)
            high, low = split3(block[0])
            parts[pl.ds(start, rows), :] = high
            parts[pl.ds(start + size, rows), :] = low
            parts[pl.ds(start + 2 * size, rows), :] = high


def early_kernel(me_ref, op_ref, *refs):
    same, other = refs[:EARLY], refs[EARLY : 2 * EARLY]
    out_ref, parts = refs[2 * EARLY :]
    load_parts(me_ref[0] & 1, same, other, parts)
    out_ref[0] = jnp.dot(op_ref[...], parts[...], preferred_element_type=jnp.float32)


def early_lines(me, operators, same, other):
    fields = same[0].shape[0] - 1
    rows, width = same[0].shape[1:]
    height, size = operators.shape
    piece = pl.BlockSpec((1, rows, width), lambda f, me: (f, 0, 0))
    return pl.pallas_call(
        early_kernel,
        grid_spec=pltpu.PrefetchScalarGridSpec(
            num_scalar_prefetch=1,
            grid=(fields,),
            in_specs=[pl.BlockSpec(operators.shape, lambda f, me: (0, 0))]
            + [piece] * (2 * EARLY),
            out_specs=pl.BlockSpec((1, height, width), lambda f, me: (f, 0, 0)),
            scratch_shapes=[pltpu.VMEM((size, width), jnp.bfloat16)],
        ),
        out_shape=jax.ShapeDtypeStruct((fields, height, width), jnp.float32),
        name="early_lines",
        cost_estimate=pl.CostEstimate(
            flops=2 * height * size * width * fields,
            bytes_accessed=12 * 1024 * 1024,
            transcendentals=0,
        ),
    )(me, operators, *same, *other)


def late_kernel(me_ref, coupling_ref, op_ref, sums_ref, *refs):
    count = len(OFFSETS)
    same, other = refs[:EARLY], refs[EARLY : 2 * EARLY]
    speeds = refs[2 * EARLY : 2 * EARLY + count]
    outs = refs[2 * EARLY + count : 2 * EARLY + 2 * count]
    parts, grads = refs[2 * EARLY + 2 * count :]
    field = pl.program_id(0)
    fields = pl.num_programs(0)
    rows = same[0].shape[1]
    load_parts(me_ref[0] & 1, same, other, parts)
    grads[field] = sums_ref[0] + jnp.dot(
        op_ref[...], parts[...], preferred_element_type=jnp.float32
    )

    @pl.when(field == fields - 1)
    def _():
        half = grads.shape[1] // 2
        for o in range(count):
            start = pl.multiple_of(target(me_ref[0], o) * rows, rows)
            for part in range(0, rows, 16):
                firsts = [grads[g, pl.ds(start + part, 16), :] for g in range(5)]
                speed = speeds[o][0, pl.ds(part, 16), :] * stepping
                for f in range(5):
                    second = grads[f, pl.ds(start + half + part, 16), :]
                    outs[o][f, pl.ds(part, 16), :] = (
                        speed * mixed(coupling_ref, 1, firsts, f)
                        + (viscous * stepping) * second
                    )


def late_lines(me, coupling, operators, sums, same, other, everyone):
    count = len(OFFSETS)
    fields = same[0].shape[0] - 1
    rows, width = same[0].shape[1:]
    height, size = operators.shape
    piece = pl.BlockSpec((1, rows, width), lambda f, me: (f, 0, 0))
    last = pl.BlockSpec((1, rows, width), lambda f, me: (fields, 0, 0))
    return pl.pallas_call(
        late_kernel,
        grid_spec=pltpu.PrefetchScalarGridSpec(
            num_scalar_prefetch=1,
            grid=(fields,),
            in_specs=[
                pl.BlockSpec(memory_space=pltpu.SMEM),
                pl.BlockSpec(operators.shape, lambda f, me: (0, 0)),
                pl.BlockSpec((1, height, width), lambda f, me: (f, 0, 0)),
            ]
            + [piece] * (2 * EARLY)
            + [last] * count,
            out_specs=[pl.BlockSpec((fields, rows, width), lambda f, me: (0, 0, 0))] * count,
            scratch_shapes=[
                pltpu.VMEM((size, width), jnp.bfloat16),
                pltpu.VMEM((fields, height, width), jnp.float32),
            ],
        ),
        out_shape=[jax.ShapeDtypeStruct((fields, rows, width), jnp.float32)] * count,
        name="late_lines",
        cost_estimate=pl.CostEstimate(
            flops=2 * height * size * width * fields,
            bytes_accessed=16 * 1024 * 1024,
            transcendentals=0,
        ),
    )(me, coupling, operators, sums, *same, *other, *[everyone[m] for m in MIRRORED])


def mixed(coupling_ref, axis, grads, f):
    total = coupling_ref[0, axis, f] * grads[0]
    for g in range(1, len(grads)):
        total = total + coupling_ref[g, axis, f] * grads[g]
    return total


def edges_kernel(column_ref, adjoint_ref, top_ref, bottom_ref, near_ref, far_ref, hold, arrive, leave):
    fields, depth = adjoint_ref.shape[:2]
    half = HALO // 2
    edge = jnp.where(column_ref[0] == 3, depth - HALO, 0)

    def load(f):
        return pltpu.make_async_copy(adjoint_ref.at[f], hold.at[f], arrive.at[f])

    def stores(f):
        return [
            pltpu.make_async_copy(hold.at[f, pl.ds(start, size)], out.at[f], leave.at[f, k])
            for k, (out, start, size) in enumerate(
                (
                    (near_ref, edge, half),
                    (far_ref, edge + half, half),
                    (top_ref, depth - HALO, HALO),
                    (bottom_ref, 0, HALO),
                )
            )
        ]

    for f in range(fields):
        load(f).start()
    for f in range(fields):
        load(f).wait()
        for copy in stores(f):
            copy.start()
    for f in range(fields):
        for copy in stores(f):
            copy.wait()


def edges(column, adjoint):
    fields, _, rows, width = adjoint.shape
    counts = (HALO, HALO, HALO // 2, HALO // 2)
    anywhere = pl.BlockSpec(memory_space=pl.ANY)
    return pl.pallas_call(
        edges_kernel,
        in_specs=[pl.BlockSpec(memory_space=pltpu.SMEM), anywhere],
        out_specs=[anywhere] * len(counts),
        out_shape=[jax.ShapeDtypeStruct((fields, count, rows, width), jnp.float32) for count in counts],
        scratch_shapes=[
            pltpu.VMEM(adjoint.shape, jnp.float32),
            pltpu.SemaphoreType.DMA((fields,)),
            pltpu.SemaphoreType.DMA((fields, len(counts))),
        ],
        name="edges",
        cost_estimate=pl.CostEstimate(flops=0, bytes_accessed=7 * 1024 * 1024, transcendentals=0),
    )(column, adjoint)


def local_kernel(
    me_ref, column_ref, coupling_ref, adjoint_ref, low_ref, high_ref, near_ref, far_ref,
    speed_ref, xd_ref, *refs,
):
    parts, (out_ref, full_ref, gx_ref) = refs[:-3], refs[-3:]
    fields, depth, rows, width = adjoint_ref.shape
    half = HALO // 2
    first, last = column_ref[0] == 0, column_ref[0] == 3
    for g in range(fields):
        for k in range(HALO):
            wrapped = near_ref[g, k] if k < half else far_ref[g, k - half]
            full_ref[g, k] = jnp.where(first, wrapped, low_ref[g, k])
            full_ref[g, HALO + k] = jnp.where(last, wrapped, high_ref[g, k])
    flat = adjoint_ref[...].reshape(fields * depth * rows, width)
    fh, fl = split3(flat)
    xh, xl = split3(xd_ref[...])

    def product(a, b):
        return lax.dot_general(a, b, (((1,), (1,)), ((), ())), preferred_element_type=jnp.float32)

    grad_x = product(fh, xh) + product(fl, xh) + product(fh, xl)
    gx_ref[...] = grad_x.reshape(fields, depth, rows, width)

    def plane(g, k):
        if k < 0:
            return full_ref[g, HALO + k]
        if k >= depth:
            return full_ref[g, HALO + k - depth]
        return adjoint_ref[g, k]

    for z in range(depth):
        grads = []
        for g in range(fields):
            total = None
            for step, weight in enumerate(stencil):
                term = weight * (plane(g, z + step + 1) - plane(g, z - step - 1))
                total = term if total is None else total + term
            grads.append(total)
        firsts = [gx_ref[g, z] for g in range(fields)]
        speed = speed_ref[z] * stepping
        for f in range(fields):
            total = mixed(coupling_ref, 0, firsts, f) + mixed(coupling_ref, 2, grads, f)
            out_ref[f, z] = adjoint_ref[f, z] + speed * total
    for o, part_ref in enumerate(parts):
        plane_of = source(me_ref[0], o)
        for f in range(fields):
            out_ref[f, plane_of] = out_ref[f, plane_of] + part_ref[f]


def local_terms(me, column, coupling, adjoint, low, high, near, far, speed, x_derivative, parts):
    fields, depth, rows, width = adjoint.shape
    step = 8
    whole = pl.BlockSpec((fields, depth, step, width), lambda r: (0, 0, r, 0))
    side = pl.BlockSpec((fields, HALO, step, width), lambda r: (0, 0, r, 0))
    part = pl.BlockSpec((fields, HALO // 2, step, width), lambda r: (0, 0, r, 0))
    return pl.pallas_call(
        local_kernel,
        grid=(rows // step,),
        in_specs=[
            pl.BlockSpec(memory_space=pltpu.SMEM),
            pl.BlockSpec(memory_space=pltpu.SMEM),
            pl.BlockSpec(memory_space=pltpu.SMEM),
            whole,
            side,
            side,
            part,
            part,
            pl.BlockSpec((depth, step, width), lambda r: (0, r, 0)),
            pl.BlockSpec((width, width), lambda r: (0, 0)),
        ]
        + [pl.BlockSpec((fields, step, width), lambda r: (0, r, 0))] * len(parts),
        out_specs=whole,
        out_shape=jax.ShapeDtypeStruct(adjoint.shape, jnp.float32),
        scratch_shapes=[
            pltpu.VMEM((fields, 2 * HALO, step, width), jnp.float32),
            pltpu.VMEM((fields, depth, step, width), jnp.float32),
        ],
        name="local",
        cost_estimate=pl.CostEstimate(
            flops=6 * fields * depth * rows * width * width,
            bytes_accessed=12 * 1024 * 1024,
            transcendentals=0,
        ),
    )(me, column, coupling, adjoint, low, high, near, far, speed, x_derivative, *parts)


def join_kernel(me_ref, base_ref, *refs, where):
    parts, (out_ref, hold, extra, arrive, leave) = refs[:-5], refs[-5:]
    fields = base_ref.shape[0]

    def load(k):
        plane = source(me_ref[0], where[k])
        return pltpu.make_async_copy(base_ref.at[:, plane], hold.at[k], arrive.at[k])

    def fetch(k):
        return pltpu.make_async_copy(parts[k], extra.at[k], arrive.at[len(where) + k])

    def store(k):
        plane = source(me_ref[0], where[k])
        return pltpu.make_async_copy(hold.at[k], out_ref.at[:, plane], leave.at[k])

    for k in range(len(where)):
        load(k).start()
        fetch(k).start()
    for k in range(len(where)):
        load(k).wait()
        fetch(k).wait()
        for f in range(fields):
            hold[k, f] = hold[k, f] + extra[k, f]
        store(k).start()
    for k in range(len(where)):
        store(k).wait()


def join(me, base, parts, where):
    fields, _, rows, width = base.shape
    count = len(where)
    anywhere = pl.BlockSpec(memory_space=pl.ANY)
    return pl.pallas_call(
        functools.partial(join_kernel, where=where),
        in_specs=[pl.BlockSpec(memory_space=pltpu.SMEM), anywhere] + [anywhere] * count,
        out_specs=anywhere,
        out_shape=jax.ShapeDtypeStruct(base.shape, jnp.float32),
        scratch_shapes=[
            pltpu.VMEM((count, fields, rows, width), jnp.float32),
            pltpu.VMEM((count, fields, rows, width), jnp.float32),
            pltpu.SemaphoreType.DMA((2 * count,)),
            pltpu.SemaphoreType.DMA((count,)),
        ],
        input_output_aliases={1: 0},
        name="join",
        cost_estimate=pl.CostEstimate(
            flops=count * fields * rows * width,
            bytes_accessed=count * 1024 * 1024,
            transcendentals=0,
        ),
    )(me, base, *parts)


def shards(adjoint, speed, x_derivative, y_operators, coupling):
    _, depth, rows, _ = adjoint.shape
    chips = lax.axis_size("gy") // 2
    assert chips == depth == 8 and y_operators.shape[1] == 16 * rows
    coupling = jnp.transpose(coupling, (1, 0, 2))
    me = lax.axis_index("gy").astype(jnp.int32)[None]
    column = (lax.axis_index("gz").astype(jnp.int32) & 3)[None]
    pieces = pack(me, adjoint, speed)
    same = [pieces[0]]
    for o in range(1, 8):
        same.append(lax.ppermute(pieces[o], "gy", chip_perm(*OFFSETS[o])))
    other = []
    for o in range(8):
        other.append(lax.ppermute(same[o], "gy", CORE_SWAP))

    top, bottom, near, far = edges(column, adjoint)
    runs = [4 * r for r in range(lax.axis_size("gz") // 4)]
    near = lax.ppermute(near, "gz", [p for r in runs for p in ((r + 3, r), (r, r + 3))])
    far = lax.ppermute(far, "gz", [p for r in runs for p in ((r + 3, r + 1), (r, r + 2))])
    low = lax.ppermute(top, "gz", [(r + x, r + (x + 1) % 4) for r in runs for x in range(4)])
    high = lax.ppermute(bottom, "gz", [(r + (x + 1) % 4, r + x) for r in runs for x in range(4)])
    ends = (column[0] == 0) | (column[0] == 3)
    crossing = jnp.where(ends, near, far)
    near = lax.ppermute(crossing, "gz", [(r + x, (r ^ 4) + x) for r in runs for x in range(4)])
    far = lax.ppermute(near, "gz", [p for r in runs for p in ((r + 1, r), (r + 2, r + 3))])

    early, late = own_operators(me, y_operators, chips, rows)
    sums = early_lines(me, early, same[:EARLY], other[:EARLY])
    parts = late_lines(me, coupling, late, sums, same[EARLY:], other[EARLY:], same)
    arrived = [parts[0]]
    for o in range(1, 8):
        arrived.append(lax.ppermute(parts[o], "gy", chip_perm(*OFFSETS[o])))
    result = local_terms(
        me, column, coupling, adjoint, low, high, near, far, speed, x_derivative,
        arrived[:FIRST],
    )
    for where in LATER:
        result = join(me, result, [arrived[o] for o in where], where)
    return result


def solution(mesh):
    placed = (P(None, "gz", "gy", None), P("gz", "gy", None), P(), P(), P())

    return jax.shard_map(
        shards, mesh=mesh, in_specs=placed, out_specs=P(None, "gz", "gy", None), check_vma=False
    )
```

```python
import functools

import jax
import jax.numpy as jnp
from jax import lax
from jax.experimental import pallas as pl
from jax.experimental.pallas import tpu as pltpu
from jax.sharding import PartitionSpec as P


stencil = (0.8, -0.2, 4.0 / 105.0, -1.0 / 280.0)
viscous = 0.5
stepping = 0.5

OFFSETS = ((0, 0), (1, 0), (3, 0), (0, 1), (2, 0), (1, 1), (3, 1), (2, 1))
EARLY = 4
FIRST = 4
LATER = ((4, 5, 6), (7,))
HALO = len(stencil)


def chip_perm(dz, dy):
    pairs = []
    for i in range(16):
        z, h, c = i // 4, (i // 2) % 2, i % 2
        pairs.append((i, ((z + dz) % 4) * 4 + ((h + dy) % 2) * 2 + c))
    return pairs


CORE_SWAP = [(i, i ^ 1) for i in range(16)]
MIRRORED = [OFFSETS.index(((-dz) % 4, dy)) for dz, dy in OFFSETS]


def chip_at(me, dz, dy):
    return ((((me >> 2) + dz) & 3) << 1) | (((me >> 1) & 1) ^ dy)


def target(me, o):
    return chip_at(me, OFFSETS[o][0], OFFSETS[o][1])


def source(me, o):
    return chip_at(me, 4 - OFFSETS[o][0], OFFSETS[o][1])


def split3(value):
    high = value.astype(jnp.bfloat16)
    low = (value - high.astype(jnp.float32)).astype(jnp.bfloat16)
    return high, low


def pack_kernel(me_ref, adjoint_ref, speed_ref, *refs, which):
    count = len(which)
    outs = refs[:count]
    hold, arrive, leave = refs[count:]
    fields = adjoint_ref.shape[0]

    def loads(o):
        plane = target(me_ref[0], which[o])
        return (
            pltpu.make_async_copy(
                adjoint_ref.at[:, plane], hold.at[o, pl.ds(0, fields)], arrive.at[o, 0]
            ),
            pltpu.make_async_copy(speed_ref.at[plane], hold.at[o, fields], arrive.at[o, 1]),
        )

    for o in range(count):
        for copy in loads(o):
            copy.start()
    for o in range(count):
        for copy in loads(o):
            copy.wait()
        pltpu.make_async_copy(hold.at[o], outs[o], leave.at[o]).start()
    for o in range(count):
        pltpu.make_async_copy(hold.at[o], outs[o], leave.at[o]).wait()


def pack(me, adjoint, speed, which):
    fields, _, rows, width = adjoint.shape
    count = len(which)
    anywhere = pl.BlockSpec(memory_space=pl.ANY)
    return pl.pallas_call(
        functools.partial(pack_kernel, which=which),
        in_specs=[pl.BlockSpec(memory_space=pltpu.SMEM), anywhere, anywhere],
        out_specs=[anywhere] * count,
        out_shape=[jax.ShapeDtypeStruct((fields + 1, rows, width), jnp.float32)] * count,
        scratch_shapes=[
            pltpu.VMEM((count, fields + 1, rows, width), jnp.float32),
            pltpu.SemaphoreType.DMA((count, 2)),
            pltpu.SemaphoreType.DMA((count,)),
        ],
        name="pack",
        cost_estimate=pl.CostEstimate(flops=0, bytes_accessed=6 * 1024 * 1024, transcendentals=0),
    )(me, adjoint, speed)


def operator_kernel(
    me_ref, column_ref, op_ref, adjoint_ref, early_ref, late_ref, near_ref, far_ref, top_ref,
    bottom_ref, hold, arrive, leave,
):
    fields, depth = adjoint_ref.shape[:2]
    half = HALO // 2
    edge = jnp.where(column_ref[0] == 3, depth - HALO, 0)
    step = pl.program_id(0) * pl.num_programs(1) + pl.program_id(1)
    steps = pl.num_programs(0) * pl.num_programs(1)

    def load(f):
        return pltpu.make_async_copy(adjoint_ref.at[f], hold.at[f], arrive.at[f])

    def stores(f):
        return [
            pltpu.make_async_copy(hold.at[f, pl.ds(start, size)], out.at[f], leave.at[f, k])
            for k, (out, start, size) in enumerate(
                (
                    (near_ref, edge, half),
                    (far_ref, edge + half, half),
                    (top_ref, depth - HALO, HALO),
                    (bottom_ref, 0, HALO),
                )
            )
        ]

    @pl.when(step == 0)
    def _():
        for f in range(fields):
            load(f).start()

    @pl.when(step == 1)
    def _():
        for f in range(fields):
            load(f).wait()
        for f in range(fields):
            for copy in stores(f):
                copy.start()

    @pl.when(step == steps - 1)
    def _():
        for f in range(fields):
            for copy in stores(f):
                copy.wait()

    chips = op_ref.shape[1]
    pair = op_ref.shape[4] // 8
    size = EARLY * pair
    for t in range(chips):
        for o in range(len(OFFSETS)):
            start = pl.multiple_of(source(me_ref[0], o) * pair, pair)
            high, low = split3(op_ref[0, t, 0, :, pl.ds(start, pair)])
            out_ref = early_ref if o < EARLY else late_ref
            at = (o % EARLY) * pair
            out_ref[0, t, :, at : at + pair] = high
            out_ref[0, t, :, size + at : size + at + pair] = high
            out_ref[0, t, :, 2 * size + at : 2 * size + at + pair] = low


def prepare(me, column, y_operators, adjoint):
    ops, size, _ = y_operators.shape
    fields, chips, rows, width = adjoint.shape
    counts = (HALO // 2, HALO // 2, HALO, HALO)
    anywhere = pl.BlockSpec(memory_space=pl.ANY)
    shaped = y_operators.reshape(ops, chips, 2, rows, size)
    wide = 3 * size // 2
    step = 4
    out_spec = pl.BlockSpec((1, step, rows, wide), lambda o, t, me: (o, t, 0, 0))
    early, late, *sides = pl.pallas_call(
        operator_kernel,
        grid_spec=pltpu.PrefetchScalarGridSpec(
            num_scalar_prefetch=1,
            grid=(ops, chips // step),
            in_specs=[
                pl.BlockSpec(memory_space=pltpu.SMEM),
                pl.BlockSpec(
                    (1, step, 1, rows, size), lambda o, t, me: (o, t, me[0] & 1, 0, 0)
                ),
                anywhere,
            ],
            out_specs=[out_spec] * 2 + [anywhere] * len(counts),
            scratch_shapes=[
                pltpu.VMEM(adjoint.shape, jnp.float32),
                pltpu.SemaphoreType.DMA((fields,)),
                pltpu.SemaphoreType.DMA((fields, len(counts))),
            ],
        ),
        out_shape=[jax.ShapeDtypeStruct((ops, chips, rows, wide), jnp.bfloat16)] * 2
        + [jax.ShapeDtypeStruct((fields, count, rows, width), jnp.float32) for count in counts],
        name="operators",
        cost_estimate=pl.CostEstimate(
            flops=4 * 1024 * 1024, bytes_accessed=10 * 1024 * 1024, transcendentals=0
        ),
    )(me, column, shaped, adjoint)
    flat = (ops * chips * rows, wide)
    return early.reshape(flat), late.reshape(flat), sides


def load_parts(core, same, other, parts):
    rows = same[0].shape[1]
    size = parts.shape[0] // 3
    for o in range(EARLY):
        for block, which in ((same[o], core), (other[o], 1 - core)):
            start = pl.multiple_of(o * 2 * rows + which * rows, rows)
            high, low = split3(block[0])
            parts[pl.ds(start, rows), :] = high
            parts[pl.ds(start + size, rows), :] = low
            parts[pl.ds(start + 2 * size, rows), :] = high


def early_kernel(me_ref, op_ref, *refs):
    same, other = refs[:EARLY], refs[EARLY : 2 * EARLY]
    out_ref, parts = refs[2 * EARLY :]
    load_parts(me_ref[0] & 1, same, other, parts)
    out_ref[0] = jnp.dot(op_ref[...], parts[...], preferred_element_type=jnp.float32)


def early_lines(me, operators, same, other):
    fields = same[0].shape[0] - 1
    rows, width = same[0].shape[1:]
    height, size = operators.shape
    piece = pl.BlockSpec((1, rows, width), lambda f, me: (f, 0, 0))
    return pl.pallas_call(
        early_kernel,
        grid_spec=pltpu.PrefetchScalarGridSpec(
            num_scalar_prefetch=1,
            grid=(fields,),
            in_specs=[pl.BlockSpec(operators.shape, lambda f, me: (0, 0))]
            + [piece] * (2 * EARLY),
            out_specs=pl.BlockSpec((1, height, width), lambda f, me: (f, 0, 0)),
            scratch_shapes=[pltpu.VMEM((size, width), jnp.bfloat16)],
        ),
        out_shape=jax.ShapeDtypeStruct((fields, height, width), jnp.float32),
        name="early_lines",
        cost_estimate=pl.CostEstimate(
            flops=2 * height * size * width * fields,
            bytes_accessed=12 * 1024 * 1024,
            transcendentals=0,
        ),
    )(me, operators, *same, *other)


def late_kernel(me_ref, coupling_ref, op_ref, sums_ref, *refs):
    count = len(OFFSETS)
    same, other = refs[:EARLY], refs[EARLY : 2 * EARLY]
    speeds = refs[2 * EARLY : 2 * EARLY + count]
    outs = refs[2 * EARLY + count : 2 * EARLY + 2 * count]
    parts, grads, ready, leave = refs[2 * EARLY + 2 * count :]
    field = pl.program_id(0)
    fields = pl.num_programs(0)
    rows = same[0].shape[1]
    load_parts(me_ref[0] & 1, same, other, parts)
    grads[field] = sums_ref[0] + jnp.dot(
        op_ref[...], parts[...], preferred_element_type=jnp.float32
    )

    @pl.when(field == fields - 1)
    def _():
        half = grads.shape[1] // 2
        order = list(range(1, count)) + [0]
        for o in order:
            start = pl.multiple_of(target(me_ref[0], o) * rows, rows)
            for part in range(0, rows, 16):
                firsts = [grads[g, pl.ds(start + part, 16), :] for g in range(5)]
                speed = speeds[o][0, pl.ds(part, 16), :] * stepping
                for f in range(5):
                    second = grads[f, pl.ds(start + half + part, 16), :]
                    ready[o, f, pl.ds(part, 16), :] = (
                        speed * mixed(coupling_ref, 1, firsts, f)
                        + (viscous * stepping) * second
                    )
            pltpu.make_async_copy(ready.at[o], outs[o], leave.at[o]).start()
        for o in order:
            pltpu.make_async_copy(ready.at[o], outs[o], leave.at[o]).wait()


def late_lines(me, coupling, operators, sums, same, other, everyone):
    count = len(OFFSETS)
    fields = same[0].shape[0] - 1
    rows, width = same[0].shape[1:]
    height, size = operators.shape
    piece = pl.BlockSpec((1, rows, width), lambda f, me: (f, 0, 0))
    last = pl.BlockSpec((1, rows, width), lambda f, me: (fields, 0, 0))
    return pl.pallas_call(
        late_kernel,
        grid_spec=pltpu.PrefetchScalarGridSpec(
            num_scalar_prefetch=1,
            grid=(fields,),
            in_specs=[
                pl.BlockSpec(memory_space=pltpu.SMEM),
                pl.BlockSpec(operators.shape, lambda f, me: (0, 0)),
                pl.BlockSpec((1, height, width), lambda f, me: (f, 0, 0)),
            ]
            + [piece] * (2 * EARLY)
            + [last] * count,
            out_specs=[pl.BlockSpec(memory_space=pl.ANY)] * count,
            scratch_shapes=[
                pltpu.VMEM((size, width), jnp.bfloat16),
                pltpu.VMEM((fields, height, width), jnp.float32),
                pltpu.VMEM((count, fields, rows, width), jnp.float32),
                pltpu.SemaphoreType.DMA((count,)),
            ],
        ),
        out_shape=[jax.ShapeDtypeStruct((fields, rows, width), jnp.float32)] * count,
        name="late_lines",
        cost_estimate=pl.CostEstimate(
            flops=2 * height * size * width * fields,
            bytes_accessed=16 * 1024 * 1024,
            transcendentals=0,
        ),
    )(me, coupling, operators, sums, *same, *other, *[everyone[m] for m in MIRRORED])


def mixed(coupling_ref, axis, grads, f):
    total = coupling_ref[0, axis, f] * grads[0]
    for g in range(1, len(grads)):
        total = total + coupling_ref[g, axis, f] * grads[g]
    return total


def local_kernel(
    me_ref, column_ref, coupling_ref, adjoint_ref, low_ref, high_ref, near_ref, far_ref,
    speed_ref, xd_ref, *refs,
):
    parts, (out_ref, full_ref, gx_ref) = refs[:-3], refs[-3:]
    fields, depth, rows, width = adjoint_ref.shape
    half = HALO // 2
    first, last = column_ref[0] == 0, column_ref[0] == 3
    for g in range(fields):
        for k in range(HALO):
            wrapped = near_ref[g, k] if k < half else far_ref[g, k - half]
            full_ref[g, k] = jnp.where(first, wrapped, low_ref[g, k])
            full_ref[g, HALO + k] = jnp.where(last, wrapped, high_ref[g, k])
    flat = adjoint_ref[...].reshape(fields * depth * rows, width)
    fh, fl = split3(flat)
    xh, xl = split3(xd_ref[...])

    def product(a, b):
        return lax.dot_general(a, b, (((1,), (1,)), ((), ())), preferred_element_type=jnp.float32)

    grad_x = product(fh, xh) + product(fl, xh) + product(fh, xl)
    gx_ref[...] = grad_x.reshape(fields, depth, rows, width)

    def plane(g, k):
        if k < 0:
            return full_ref[g, HALO + k]
        if k >= depth:
            return full_ref[g, HALO + k - depth]
        return adjoint_ref[g, k]

    for z in range(depth):
        grads = []
        for g in range(fields):
            total = None
            for step, weight in enumerate(stencil):
                term = weight * (plane(g, z + step + 1) - plane(g, z - step - 1))
                total = term if total is None else total + term
            grads.append(total)
        firsts = [gx_ref[g, z] for g in range(fields)]
        speed = speed_ref[z] * stepping
        for f in range(fields):
            total = mixed(coupling_ref, 0, firsts, f) + mixed(coupling_ref, 2, grads, f)
            out_ref[f, z] = adjoint_ref[f, z] + speed * total
    for o, part_ref in enumerate(parts):
        plane_of = source(me_ref[0], o)
        for f in range(fields):
            out_ref[f, plane_of] = out_ref[f, plane_of] + part_ref[f]


def local_terms(me, column, coupling, adjoint, low, high, near, far, speed, x_derivative, parts):
    fields, depth, rows, width = adjoint.shape
    step = 8
    whole = pl.BlockSpec((fields, depth, step, width), lambda r: (0, 0, r, 0))
    side = pl.BlockSpec((fields, HALO, step, width), lambda r: (0, 0, r, 0))
    part = pl.BlockSpec((fields, HALO // 2, step, width), lambda r: (0, 0, r, 0))
    return pl.pallas_call(
        local_kernel,
        grid=(rows // step,),
        in_specs=[
            pl.BlockSpec(memory_space=pltpu.SMEM),
            pl.BlockSpec(memory_space=pltpu.SMEM),
            pl.BlockSpec(memory_space=pltpu.SMEM),
            whole,
            side,
            side,
            part,
            part,
            pl.BlockSpec((depth, step, width), lambda r: (0, r, 0)),
            pl.BlockSpec((width, width), lambda r: (0, 0)),
        ]
        + [pl.BlockSpec((fields, step, width), lambda r: (0, r, 0))] * len(parts),
        out_specs=whole,
        out_shape=jax.ShapeDtypeStruct(adjoint.shape, jnp.float32),
        scratch_shapes=[
            pltpu.VMEM((fields, 2 * HALO, step, width), jnp.float32),
            pltpu.VMEM((fields, depth, step, width), jnp.float32),
        ],
        name="local",
        cost_estimate=pl.CostEstimate(
            flops=6 * fields * depth * rows * width * width,
            bytes_accessed=12 * 1024 * 1024,
            transcendentals=0,
        ),
    )(me, column, coupling, adjoint, low, high, near, far, speed, x_derivative, *parts)


def join_kernel(me_ref, base_ref, *refs, where):
    parts, (out_ref, hold, extra, arrive, leave) = refs[:-5], refs[-5:]
    fields = base_ref.shape[0]

    def load(k):
        plane = source(me_ref[0], where[k])
        return pltpu.make_async_copy(base_ref.at[:, plane], hold.at[k], arrive.at[k])

    def fetch(k):
        return pltpu.make_async_copy(parts[k], extra.at[k], arrive.at[len(where) + k])

    def store(k):
        plane = source(me_ref[0], where[k])
        return pltpu.make_async_copy(hold.at[k], out_ref.at[:, plane], leave.at[k])

    for k in range(len(where)):
        load(k).start()
        fetch(k).start()
    for k in range(len(where)):
        load(k).wait()
        fetch(k).wait()
        for f in range(fields):
            hold[k, f] = hold[k, f] + extra[k, f]
        store(k).start()
    for k in range(len(where)):
        store(k).wait()


def join(me, base, parts, where):
    fields, _, rows, width = base.shape
    count = len(where)
    anywhere = pl.BlockSpec(memory_space=pl.ANY)
    return pl.pallas_call(
        functools.partial(join_kernel, where=where),
        in_specs=[pl.BlockSpec(memory_space=pltpu.SMEM), anywhere] + [anywhere] * count,
        out_specs=anywhere,
        out_shape=jax.ShapeDtypeStruct(base.shape, jnp.float32),
        scratch_shapes=[
            pltpu.VMEM((count, fields, rows, width), jnp.float32),
            pltpu.VMEM((count, fields, rows, width), jnp.float32),
            pltpu.SemaphoreType.DMA((2 * count,)),
            pltpu.SemaphoreType.DMA((count,)),
        ],
        input_output_aliases={1: 0},
        name="join",
        cost_estimate=pl.CostEstimate(
            flops=count * fields * rows * width,
            bytes_accessed=count * 1024 * 1024,
            transcendentals=0,
        ),
    )(me, base, *parts)


def shards(adjoint, speed, x_derivative, y_operators, coupling):
    _, depth, rows, _ = adjoint.shape
    chips = lax.axis_size("gy") // 2
    assert chips == depth == 8 and y_operators.shape[1] == 16 * rows
    coupling = jnp.transpose(coupling, (1, 0, 2))
    me = lax.axis_index("gy").astype(jnp.int32)[None]
    column = (lax.axis_index("gz").astype(jnp.int32) & 3)[None]
    *pieces, own = pack(me, adjoint, speed, (1, 2, 3, 4, 5, 6, 7, 0))
    pieces = [own, *pieces]
    same = [pieces[0]]
    for o in range(1, 8):
        same.append(lax.ppermute(pieces[o], "gy", chip_perm(*OFFSETS[o])))
    other = []
    for o in range(8):
        other.append(lax.ppermute(same[o], "gy", CORE_SWAP))

    early, late, (near, far, top, bottom) = prepare(me, column, y_operators, adjoint)
    runs = [4 * r for r in range(lax.axis_size("gz") // 4)]
    near = lax.ppermute(near, "gz", [p for r in runs for p in ((r + 3, r), (r, r + 3))])
    far = lax.ppermute(far, "gz", [p for r in runs for p in ((r + 3, r + 1), (r, r + 2))])
    low = lax.ppermute(top, "gz", [(r + x, r + (x + 1) % 4) for r in runs for x in range(4)])
    high = lax.ppermute(bottom, "gz", [(r + (x + 1) % 4, r + x) for r in runs for x in range(4)])
    ends = (column[0] == 0) | (column[0] == 3)
    crossing = jnp.where(ends, near, far)
    near = lax.ppermute(crossing, "gz", [(r + x, (r ^ 4) + x) for r in runs for x in range(4)])
    far = lax.ppermute(near, "gz", [p for r in runs for p in ((r + 1, r), (r + 2, r + 3))])

    sums = early_lines(me, early, same[:EARLY], other[:EARLY])
    parts = late_lines(me, coupling, late, sums, same[EARLY:], other[EARLY:], same)
    arrived = [parts[0]]
    for o in range(1, 8):
        arrived.append(lax.ppermute(parts[o], "gy", chip_perm(*OFFSETS[o])))
    result = local_terms(
        me, column, coupling, adjoint, low, high, near, far, speed, x_derivative,
        arrived[:FIRST],
    )
    for where in LATER:
        result = join(me, result, [arrived[o] for o in where], where)
    return result


def solution(mesh):
    placed = (P(None, "gz", "gy", None), P("gz", "gy", None), P(), P(), P())

    return jax.shard_map(
        shards, mesh=mesh, in_specs=placed, out_specs=P(None, "gz", "gy", None), check_vma=False
    )
```
